32 devices in a mesh: front: 8 (over y, x, core), tile: 4 (over z).
Axes of the slice: x: 2, y: 2, z: 4, core: 2. Of those that a mesh axis runs over, the one named last changes fastest.
Arguments:
- pivot_inverse: float32 [8, 2, 512, 512], P('front', None, 'tile'), may hold values from -0.26516504 to 0.26516504
- panel_upper: float32 [8, 2, 512, 2048], P('front', None, None, 'tile'), may hold values from -6 to 6
- panel_lower: float32 [8, 2, 2048, 512], P('front', None, 'tile'), may hold values from -4.2426407 to 4.2426407
- index_map: int32 [8, 2, 2048], replicated, may hold values from 0 to 4095, as said below
- parent_base: float32 [8, 4096, 4096], P('front', None, 'tile'), may hold values from -512 to 512
Outputs:
- parent_front: float32 [8, 4096, 4096], P('front', None, 'tile')
The draws below stay inside these ranges and needn't reach their ends.
Inputs may be any that keep to these rules, and one draw needn't show every extreme that they name: Each list index_map[g, c] holds 2048 distinct parent indices in no particular order, among them 0 and 4095.
All inputs are finite; a program needn't handle non-finite values.
Results may differ from the reference program's by a relative error of at most 0.0003.
Values sent between devices are 32-bit elements; how exact they have to be, the bound alone decides.
A program may use at most 128 MiB of HBM per device.

```python
import jax
import jax.numpy as jnp
from jax import lax

NP = 512
NC = 2048
NPF = 4096
CHILDREN = 2
GROUPS = 8


lower_gain = 16.0


def float_values(key, label, shape, scale):
    sub = jax.random.fold_in(key, label)
    values = jnp.clip(jax.random.normal(sub, shape, jnp.float32), -6.0, 6.0)
    return values * scale


def draw_pivot_inverse(key, part):
    return float_values(key, 11, (GROUPS, CHILDREN, NP, NP), NP ** (-0.5))


def draw_panel_upper(key, part):
    return float_values(key, 12, (GROUPS, CHILDREN, NP, NC), 1.0)


def draw_panel_lower(key, part):
    return float_values(key, 13, (GROUPS, CHILDREN, NC, NP), lower_gain * NP ** (-0.5))


def draw_index_map(key, part):
    keys = jax.random.split(jax.random.fold_in(key, 14), GROUPS * CHILDREN)

    def one_list(single):
        first_key, second_key = jax.random.split(single)
        shuffled = jax.random.permutation(first_key, NPF - 2) + 1
        chosen = shuffled[:NC - 2].astype(jnp.int32)
        first = jnp.zeros((1,), jnp.int32)
        last = jnp.full((1,), NPF - 1, jnp.int32)
        joined = jnp.concatenate([first, chosen, last])
        order = jax.random.permutation(second_key, NC)
        return joined[order].astype(jnp.int32)
    lists = jax.vmap(one_list)(keys)
    return lists.reshape(GROUPS, CHILDREN, NC).astype(jnp.int32)


def exact_block(inverse, upper, lower, mapping):
    factor = jnp.dot(inverse, upper, precision=lax.Precision.HIGHEST)
    update = jnp.dot(lower, factor, precision=lax.Precision.HIGHEST)
    extended = jnp.zeros((NPF, NPF), jnp.float32)
    return extended.at[mapping[:, None], mapping[None, :]].set(update)


def draw_parent_base(key, part):
    inverse = draw_pivot_inverse(key, part)
    upper = draw_panel_upper(key, part)
    lower = draw_panel_lower(key, part)
    mapping = draw_index_map(key, part)
    noise_key = jax.random.fold_in(key, 15)

    def one_parent(group):
        partner = jnp.bitwise_xor(group, 1).astype(jnp.int32)
        first = exact_block(inverse[group, 0], upper[group, 0], lower[group, 0], mapping[group, 0])
        second = exact_block(inverse[partner, 1], upper[partner, 1], lower[partner, 1], mapping[partner, 1])
        noise = float_values(jax.random.fold_in(noise_key, group), 16, (NPF, NPF), 1.0)
        return jnp.clip(noise + first + second, -512.0, 512.0)
    groups = jnp.arange(GROUPS, dtype=jnp.int32)
    return lax.map(one_parent, groups)


def setup_inputs(seed: int = 0) -> dict:
    key_of = jax.random.split(jax.random.key(seed), 6)
    pivot_inverse = draw_pivot_inverse(jax.random.fold_in(key_of[5], 71), 0)
    panel_upper = draw_panel_upper(jax.random.fold_in(key_of[5], 71), 0)
    panel_lower = draw_panel_lower(jax.random.fold_in(key_of[5], 71), 0)
    index_map = draw_index_map(jax.random.fold_in(key_of[5], 71), 0)
    parent_base = draw_parent_base(jax.random.fold_in(key_of[5], 71), 0)
    return {"pivot_inverse": pivot_inverse, "panel_upper": panel_upper, "panel_lower": panel_lower, "index_map": index_map, "parent_base": parent_base}


def split_parts(matrix):
    high = matrix.astype(jnp.bfloat16)
    back = lax.optimization_barrier(high).astype(jnp.float32)
    low = (matrix - back).astype(jnp.bfloat16)
    return high, low


def split_product(left, right):
    left_high, left_low = split_parts(left)
    right_high, right_low = split_parts(right)
    total = jnp.dot(left_high, right_high, preferred_element_type=jnp.float32)
    total = total + jnp.dot(left_high, right_low, preferred_element_type=jnp.float32)
    return total + jnp.dot(left_low, right_high, preferred_element_type=jnp.float32)


def child_block(pivot_inverse, panel_upper, panel_lower, index_map, group, child):
    inverse = pivot_inverse[group, child]
    upper = panel_upper[group, child]
    lower = panel_lower[group, child]
    mapping = index_map[group, child].astype(jnp.int32)
    factor = split_product(inverse, upper)
    update = split_product(lower, factor)
    return place_update(mapping, update)


def place_update(mapping, update):
    extended = jnp.zeros((NPF, NPF), jnp.float32)
    return extended.at[mapping[:, None], mapping[None, :]].set(update)


def reference(pivot_inverse, panel_upper, panel_lower, index_map, parent_base):
    def one_parent(group):
        partner = jnp.bitwise_xor(group, 1).astype(jnp.int32)
        first = child_block(pivot_inverse, panel_upper, panel_lower, index_map, group, 0)
        second = child_block(pivot_inverse, panel_upper, panel_lower, index_map, partner, 1)
        return parent_base[group] - first - second

    groups = jnp.arange(parent_base.shape[0], dtype=jnp.int32)
    return lax.map(one_parent, groups)
```

```python
import jax
import jax.numpy as jnp
from jax import lax
from jax.sharding import PartitionSpec as P


def partner_2(value, axis, distance):
    mask = 2**distance
    pairs = [(source, source ^ mask) for source in range(lax.axis_size(axis))]
    return lax.ppermute(value, axis, pairs)


def split_parts(matrix):
    high = matrix.astype(jnp.bfloat16)
    back = lax.optimization_barrier(high).astype(jnp.float32)
    low = (matrix - back).astype(jnp.bfloat16)
    return (high, low)


def dot(left, right):
    return jnp.dot(left, right, preferred_element_type=jnp.float32)


def split_product(left, right):
    left_high, left_low = left
    right_high, right_low = right
    total = dot(left_high, right_high)
    total = total + dot(left_high, right_low)
    return total + dot(left_low, right_high)


def line_gather(own, size, first, last):
    right = [own]
    left = [own]
    for step in range(1, size):
        ahead = [(i, i + 1) for i in range(step - 1, size - 1) if i + 1 <= last]
        back = [(i, i - 1) for i in range(1, size - step + 1) if i - 1 >= first]
        right.append(lax.ppermute(right[-1], "tile", ahead) if ahead else None)
        left.append(lax.ppermute(left[-1], "tile", back) if back else None)
    tile = lax.axis_index("tile")
    blocks = []
    for d in range(1, size):
        a, b = left[d], right[size - d]
        if a is None or b is None:
            blocks.append(b if a is None else a)
        else:
            blocks.append(jnp.where(tile + d < size, a, b))
    return blocks


def shards(pivot_inverse, panel_upper, panel_lower, index_map, parent_base):
    base = parent_base[0]
    order, width = base.shape
    size = lax.axis_size("tile")
    tile = lax.axis_index("tile")
    group = lax.axis_index("front")
    partner = jnp.bitwise_xor(group, 1)
    pivots = pivot_inverse.shape[3]
    rows = panel_lower.shape[2]
    at_end = (tile == 0) | (tile == size - 1)

    far = partner_2((pivot_inverse[0, 1], panel_upper[0, 1], panel_lower[0, 1]), "front", 0)
    inverses = (pivot_inverse[0, 0], far[0])
    uppers = (panel_upper[0, 0], far[1])
    lowers = (panel_lower[0, 0], far[2])
    maps = (
        lax.dynamic_index_in_dim(index_map, group, 0, keepdims=False)[0],
        lax.dynamic_index_in_dim(index_map, partner, 0, keepdims=False)[1],
    )
    end_start = jnp.where(tile * 2 < size, 0, (size - 1) * width)
    columns = jnp.concatenate(
        [jnp.arange(width, dtype=jnp.int32) + tile * width, jnp.arange(width, dtype=jnp.int32) + end_start]
    )

    upper_parts, inverse_parts = [], []
    for child in range(2):
        inverse_rot = jnp.concatenate(
            [inverses[child]] + line_gather(inverses[child], size, 1, size - 2), axis=0
        )
        full = jnp.roll(inverse_rot, tile * inverses[child].shape[0], axis=0)
        inverse_parts.append(split_parts(full))
        upper_rot = jnp.concatenate(
            [uppers[child]] + line_gather(uppers[child], size, 1, size - 2), axis=1
        )
        upper_parts.append(split_parts(upper_rot))
    lower_rots = [
        jnp.concatenate([lowers[child]] + line_gather(lowers[child], size, 0, size - 1), axis=0)
        for child in range(2)
    ]

    result = base
    for child in range(2):
        rolled = jnp.roll(maps[child], -tile * rows)
        choose = (rolled[:, None] == columns[None, :]).astype(jnp.bfloat16)
        picked = tuple(dot(part, choose).astype(jnp.bfloat16) for part in upper_parts[child])
        factor = split_product(inverse_parts[child], picked)
        pairs = [(size - 2, size - 1), (1, 0)]
        received = lax.ppermute(factor[:, width:], "tile", pairs)
        factor_ext = split_parts(jnp.where(at_end, received, factor[:, :width]))
        place = (jnp.arange(order, dtype=jnp.int32)[:, None] == rolled[None, :]).astype(jnp.bfloat16)
        lower_ext = tuple(
            dot(place, part).astype(jnp.bfloat16) for part in split_parts(lower_rots[child])
        )
        result = result - split_product(lower_ext, factor_ext)
    return result[None]


def solution(mesh):
    return jax.shard_map(
        shards,
        mesh=mesh,
        in_specs=(
            P("front", None, "tile", None),
            P("front", None, None, "tile"),
            P("front", None, "tile", None),
            P(),
            P("front", None, "tile"),
        ),
        out_specs=P("front", None, "tile"),
        check_vma=False,
    )
```

```python
import functools

import jax
import jax.numpy as jnp
from jax import lax
from jax.experimental import pallas as pl
from jax.experimental.pallas import tpu as pltpu
from jax.sharding import PartitionSpec as P

MESH = pl.DeviceIdType.MESH


def parts(value):
    high = value.astype(jnp.bfloat16)
    return high, (value - high.astype(jnp.float32)).astype(jnp.bfloat16)


def dot(left, right, contract=(1, 0)):
    dims = (((contract[0],), (contract[1],)), ((), ()))
    return lax.dot_general(left, right, dims, preferred_element_type=jnp.float32)


def split_product(left, right):
    total = dot(left[0], right[0])
    total = total + dot(left[0], right[1])
    return total + dot(left[1], right[0])


def update_kernel(
    n, inv_in, up_in, low_in, map_ref, u_out,
    up, inv, low, up_h, up_l, inv_h, inv_l, f_end, f_own, f_h, f_l, stage,
    local_sem, part_send, part_recv, up_send, up_recv, inv_send, inv_recv,
    low_send, low_recv, f_send, f_recv, out_sem,
):
    t = lax.axis_index("tile")
    f = lax.axis_index("front")
    partner = lax.rem(f, 2) * -2 + 1 + f
    count = map_ref.shape[2]
    wc = up.shape[3]
    kr = inv.shape[2]
    width = f_own.shape[2]
    chunk = min(256, width)
    middle = (t >= 1) & (t <= n - 2)
    at_end = (t == 0) | (t == n - 1)

    barrier = pltpu.get_barrier_semaphore()
    pl.semaphore_signal(barrier, inc=1, device_id=(partner, t), device_id_type=MESH)

    @pl.when(t > 0)
    def _():
        pl.semaphore_signal(barrier, inc=1, device_id=(f, t - 1), device_id_type=MESH)

    @pl.when(t < n - 1)
    def _():
        pl.semaphore_signal(barrier, inc=1, device_id=(f, t + 1), device_id_type=MESH)

    @pl.when(at_end)
    def _():
        pl.semaphore_wait(barrier, 2)

    @pl.when(middle)
    def _():
        pl.semaphore_wait(barrier, 3)

    sources = (up_in, inv_in, low_in)
    targets = (up, inv, low)

    def local(kind):
        return pltpu.make_async_copy(sources[kind].at[0], targets[kind].at[0, t], local_sem.at[kind])

    def exchange(kind):
        return pltpu.make_async_remote_copy(
            src_ref=sources[kind].at[1], dst_ref=targets[kind].at[1, t],
            send_sem=part_send.at[kind], recv_sem=part_recv.at[kind],
            device_id=(partner, t), device_id_type=MESH,
        )

    def hop(kind, child, shard, side):
        send, recv = ((up_send, up_recv), (inv_send, inv_recv), (low_send, low_recv))[kind]
        ref = targets[kind].at[child, shard]
        return pltpu.make_async_remote_copy(
            src_ref=ref, dst_ref=ref,
            send_sem=send.at[side, child, shard], recv_sem=recv.at[child, shard],
            device_id=(f, lax.rem(t + (1 if side == 0 else n - 1), n)), device_id_type=MESH,
        )

    def takes(kind, side):
        if kind == 2:
            return t + 1 <= n - 1 if side == 0 else t - 1 >= 0
        return t + 1 <= n - 2 if side == 0 else t - 1 >= 1

    def send(kind, child, shard, side):
        @pl.when(takes(kind, side))
        def _():
            hop(kind, child, shard, side).start()

    def send_own(kind, child):
        send(kind, child, t, 0)
        send(kind, child, t, 1)

    def relay(kinds, child, d):
        for side, shard, valid in ((0, t - d, t - d >= 0), (1, t + d, t + d <= n - 1)):
            @pl.when(valid & (middle if 0 in kinds else t >= 0))
            def _():
                for kind in kinds:
                    hop(kind, child, shard, side).wait_recv()
                    send(kind, child, shard, side)

    def split_child(child):
        @pl.loop(0, n)
        def _(s):
            high, low_part = parts(up[child, s])
            up_h[s] = high
            up_l[s] = low_part
            rows = pl.ds(pl.multiple_of(s * kr, kr), kr)
            high, low_part = parts(inv[child, s])
            inv_h[rows, :] = high
            inv_l[rows, :] = low_part

    def factor(child, start, dst):
        @pl.loop(0, width // chunk)
        def _(j):
            base = pl.multiple_of(j * chunk, chunk)
            columns = lax.broadcasted_iota(jnp.int32, (chunk, wc), 0) + (start + base)
            high = low_part = None
            for s in range(n):
                listed = map_ref[child, :, s * wc:(s + 1) * wc]
                choose = (columns == listed).astype(jnp.float32).astype(jnp.bfloat16)
                a = dot(up_h[s], choose, (1, 1))
                b = dot(up_l[s], choose, (1, 1))
                high = a if high is None else high + a
                low_part = b if low_part is None else low_part + b
            picked = (high.astype(jnp.bfloat16), low_part.astype(jnp.bfloat16))
            dst[child, :, pl.ds(base, chunk)] = split_product((inv_h[...], inv_l[...]), picked)

    def end_copy(child, side):
        return pltpu.make_async_remote_copy(
            src_ref=f_end.at[child], dst_ref=f_own.at[child],
            send_sem=f_send.at[child], recv_sem=f_recv.at[child],
            device_id=(f, lax.rem(t + (1 if side == 0 else n - 1), n)), device_id_type=MESH,
        )

    def serve(child):
        @pl.when(middle)
        def _():
            split_child(child)

            @pl.when(t == n - 2)
            def _():
                factor(child, (n - 1) * width, f_end)
                end_copy(child, 0).start()

            @pl.when(t == 1)
            def _():
                factor(child, 0, f_end)
                end_copy(child, 1).start()

            factor(child, t * width, f_own)

    def split_factor(child):
        @pl.when(at_end)
        def _():
            end_copy(child, 0).wait_recv()

        @pl.loop(0, width // chunk)
        def _(j):
            cols = pl.ds(pl.multiple_of(j * chunk, chunk), chunk)
            high, low_part = parts(f_own[child, :, cols])
            f_h[child, :, cols] = high
            f_l[child, :, cols] = low_part

    def put(child, shard):
        left = parts(low[child, shard])

        @pl.loop(0, width // chunk)
        def _(j):
            cols = pl.ds(pl.multiple_of(j * chunk, chunk), chunk)
            stage[:, cols] = split_product(left, (f_h[child, :, cols], f_l[child, :, cols]))

        copy = pltpu.make_async_copy(stage, u_out.at[child, shard], out_sem)
        copy.start()
        copy.wait()

    for kind in range(3):
        exchange(kind).start()
        local(kind).start()
    for kind in range(3):
        local(kind).wait()
    send_own(0, 0)
    send_own(1, 0)

    @pl.when(t == n - 2)
    def _():
        hop(2, 0, t, 0).start()

    @pl.when(t == 1)
    def _():
        hop(2, 0, t, 1).start()

    for kind in range(3):
        exchange(kind).wait()

    @pl.when(t == n - 2)
    def _():
        hop(2, 1, t, 0).start()

    @pl.when(t == 1)
    def _():
        hop(2, 1, t, 1).start()

    @pl.loop(1, n)
    def _(d):
        relay((0, 1), 0, d)

    send_own(0, 1)
    send_own(1, 1)
    serve(0)

    @pl.loop(1, n)
    def _(d):
        relay((0, 1), 1, d)

    for child in range(2):
        @pl.when((t < n - 1) & (t != n - 2))
        def _():
            hop(2, child, t, 0).start()

        @pl.when((t > 0) & (t != 1))
        def _():
            hop(2, child, t, 1).start()

    serve(1)
    for child in range(2):
        split_factor(child)

    @pl.loop(0, 2)
    def _(child):
        put(child, t)

    @pl.loop(1, n)
    def _(d):
        for child in range(2):
            relay((2,), child, d)

        @pl.loop(0, 2)
        def _(child):
            @pl.when(t - d >= 0)
            def _():
                put(child, t - d)

            @pl.when(t + d <= n - 1)
            def _():
                put(child, t + d)

    for child in range(2):
        @pl.loop(0, n)
        def _(s):
            for side in range(2):
                for kind in range(3):
                    @pl.when(takes(kind, side) & (s <= t if side == 0 else s >= t))
                    def _():
                        hop(kind, child, s, side).wait_send()

        @pl.when((t == n - 2) | (t == 1))
        def _():
            end_copy(child, 0).wait_send()


def gathered_updates(inverse, upper, lower, maps, n, width):
    pivots = inverse.shape[2]
    kr, wc, lr = inverse.shape[1], upper.shape[2], lower.shape[1]
    vmem = pltpu.VMEM
    dma = pltpu.SemaphoreType.DMA
    f32, b16 = jnp.float32, jnp.bfloat16
    return pl.pallas_call(
        functools.partial(update_kernel, n),
        out_shape=jax.ShapeDtypeStruct((2, n, lr, width), f32),
        in_specs=[pl.BlockSpec(memory_space=pl.ANY)] * 3 + [pl.BlockSpec(memory_space=vmem)],
        out_specs=pl.BlockSpec(memory_space=pl.ANY),
        scratch_shapes=[
            vmem((2, n, pivots, wc), f32),
            vmem((2, n, kr, pivots), f32),
            vmem((2, n, lr, pivots), f32),
            vmem((n, pivots, wc), b16),
            vmem((n, pivots, wc), b16),
            vmem((n * kr, pivots), b16),
            vmem((n * kr, pivots), b16),
            vmem((2, pivots, width), f32),
            vmem((2, pivots, width), f32),
            vmem((2, pivots, width), b16),
            vmem((2, pivots, width), b16),
            vmem((lr, width), f32),
            dma((3,)), dma((3,)), dma((3,)),
            dma((2, 2, n)), dma((2, n)),
            dma((2, 2, n)), dma((2, n)),
            dma((2, 2, n)), dma((2, n)),
            dma((2,)), dma((2,)), dma,
        ],
        compiler_params=pltpu.CompilerParams(
            collective_id=0, has_side_effects=True, vmem_limit_bytes=56 * 1024 * 1024
        ),
    )(inverse, upper, lower, maps)


def place_kernel(first_ref, second_ref, base_ref, u_ref, out_ref, u, rows, sem):
    block = base_ref.shape[0]
    total = u_ref.shape[0]
    start = pl.program_id(0) * block

    @pl.when(pl.program_id(0) == 0)
    def _():
        copy = pltpu.make_async_copy(u_ref, u.at[pl.ds(0, total)], sem)
        copy.start()
        u[pl.ds(total, 8), :] = jnp.zeros((8, u.shape[1]), jnp.float32)
        copy.wait()

    @pl.loop(0, block // 8)
    def _(i):
        for j in range(8):
            r = i * 8 + j
            a = u[pl.ds(first_ref[start + r], 1), :]
            b = u[pl.ds(second_ref[start + r], 1), :]
            rows[pl.ds(r, 1), :] = a + b

    out_ref[...] = base_ref[...] - rows[...]


def placed(base, updates, first, second):
    order, width = base.shape
    block = 256
    return pl.pallas_call(
        place_kernel,
        out_shape=jax.ShapeDtypeStruct(base.shape, base.dtype),
        grid_spec=pltpu.PrefetchScalarGridSpec(
            num_scalar_prefetch=2,
            grid=(order // block,),
            in_specs=[
                pl.BlockSpec((block, width), lambda i, *_: (i, 0)),
                pl.BlockSpec(memory_space=pl.ANY),
            ],
            out_specs=pl.BlockSpec((block, width), lambda i, *_: (i, 0)),
            scratch_shapes=[
                pltpu.VMEM((updates.shape[0] + 8, width), jnp.float32),
                pltpu.VMEM((block, width), jnp.float32),
                pltpu.SemaphoreType.DMA,
            ],
        ),
        compiler_params=pltpu.CompilerParams(vmem_limit_bytes=40 * 1024 * 1024),
    )(first, second, base, updates)


def shards(pivot_inverse, panel_upper, panel_lower, index_map, parent_base):
    base = parent_base[0]
    order, width = base.shape
    n = lax.axis_size("tile")
    group = lax.axis_index("front")
    partner = jnp.bitwise_xor(group, 1)
    count = index_map.shape[2]
    maps = jnp.stack([
        lax.dynamic_index_in_dim(index_map, group, 0, keepdims=False)[0],
        lax.dynamic_index_in_dim(index_map, partner, 0, keepdims=False)[1],
    ])
    updates = gathered_updates(
        pivot_inverse[0], panel_upper[0], panel_lower[0], maps[:, None, :], n, width
    )
    rows = jnp.arange(order, dtype=jnp.int32)
    listed = jnp.arange(count, dtype=jnp.int32)
    sources = []
    for child in range(2):
        hit = maps[child][None, :] == rows[:, None]
        place = jnp.max(jnp.where(hit, listed[None, :], -1), axis=1)
        sources.append(jnp.where(place >= 0, place + child * count, 2 * count))
    return placed(base, updates.reshape(2 * count, width), sources[0], sources[1])[None]


def solution(mesh):
    return jax.shard_map(
        shards,
        mesh=mesh,
        in_specs=(
            P("front", None, "tile", None),
            P("front", None, None, "tile"),
            P("front", None, "tile", None),
            P(),
            P("front", None, "tile"),
        ),
        out_specs=P("front", None, "tile"),
        check_vma=False,
    )
```

```python
import functools

import jax
import jax.numpy as jnp
from jax import lax
from jax.experimental import pallas as pl
from jax.experimental.pallas import tpu as pltpu
from jax.sharding import PartitionSpec as P

MESH = pl.DeviceIdType.MESH


def parts(value):
    high = value.astype(jnp.bfloat16)
    return high, (value - high.astype(jnp.float32)).astype(jnp.bfloat16)


def dot(left, right, contract=(1, 0)):
    dims = (((contract[0],), (contract[1],)), ((), ()))
    return lax.dot_general(left, right, dims, preferred_element_type=jnp.float32)


def split_product(left, right):
    total = dot(left[0], right[0])
    total = total + dot(left[0], right[1])
    return total + dot(left[1], right[0])


def update_kernel(
    n, inv_in, up_in, low_in, map_ref, u_out, index_out,
    up, inv, low, up_h, up_l, inv_h, inv_l, f_end, f_own, f_h, f_l, stage,
    local_sem, part_send, part_recv, up_send, up_recv, inv_send, inv_recv,
    low_send, low_recv, f_send, f_recv, out_sem,
):
    t = lax.axis_index("tile")
    f = lax.axis_index("front")
    partner = lax.rem(f, 2) * -2 + 1 + f
    count = map_ref.shape[2]
    wc = up.shape[3]
    kr = inv.shape[2]
    width = f_own.shape[2]
    chunk = min(256, width)
    middle = (t >= 1) & (t <= n - 2)
    at_end = (t == 0) | (t == n - 1)

    barrier = pltpu.get_barrier_semaphore()
    pl.semaphore_signal(barrier, inc=1, device_id=(partner, t), device_id_type=MESH)

    @pl.when(t > 0)
    def _():
        pl.semaphore_signal(barrier, inc=1, device_id=(f, t - 1), device_id_type=MESH)

    @pl.when(t < n - 1)
    def _():
        pl.semaphore_signal(barrier, inc=1, device_id=(f, t + 1), device_id_type=MESH)

    @pl.when(at_end)
    def _():
        pl.semaphore_wait(barrier, 2)

    @pl.when(middle)
    def _():
        pl.semaphore_wait(barrier, 3)

    sources = (up_in, inv_in, low_in)
    targets = (up, inv, low)

    def local(kind):
        return pltpu.make_async_copy(sources[kind].at[0], targets[kind].at[0, t], local_sem.at[kind])

    def exchange(kind):
        return pltpu.make_async_remote_copy(
            src_ref=sources[kind].at[1], dst_ref=targets[kind].at[1, t],
            send_sem=part_send.at[kind], recv_sem=part_recv.at[kind],
            device_id=(partner, t), device_id_type=MESH,
        )

    def hop(kind, child, shard, side):
        send, recv = ((up_send, up_recv), (inv_send, inv_recv), (low_send, low_recv))[kind]
        ref = targets[kind].at[child, shard]
        return pltpu.make_async_remote_copy(
            src_ref=ref, dst_ref=ref,
            send_sem=send.at[side, child, shard], recv_sem=recv.at[child, shard],
            device_id=(f, lax.rem(t + (1 if side == 0 else n - 1), n)), device_id_type=MESH,
        )

    def takes(kind, side):
        if kind == 2:
            return t + 1 <= n - 1 if side == 0 else t - 1 >= 0
        return t + 1 <= n - 2 if side == 0 else t - 1 >= 1

    def send(kind, child, shard, side):
        @pl.when(takes(kind, side))
        def _():
            hop(kind, child, shard, side).start()

    def send_own(kind, child):
        send(kind, child, t, 0)
        send(kind, child, t, 1)

    def relay(kinds, child, d):
        for side, shard, valid in ((0, t - d, t - d >= 0), (1, t + d, t + d <= n - 1)):
            @pl.when(valid & (middle if 0 in kinds else t >= 0))
            def _():
                for kind in kinds:
                    hop(kind, child, shard, side).wait_recv()
                    send(kind, child, shard, side)

    def split_child(child):
        @pl.loop(0, n)
        def _(s):
            high, low_part = parts(up[child, s])
            up_h[s] = high
            up_l[s] = low_part
            rows = pl.ds(pl.multiple_of(s * kr, kr), kr)
            high, low_part = parts(inv[child, s])
            inv_h[rows, :] = high
            inv_l[rows, :] = low_part

    def factor(child, start, dst, after):
        @pl.loop(0, width // chunk)
        def _(j):
            base = pl.multiple_of(j * chunk, chunk)
            columns = lax.broadcasted_iota(jnp.int32, (chunk, wc), 0) + (start + base)
            high = low_part = None
            for s in range(n):
                listed = map_ref[child, :, s * wc:(s + 1) * wc]
                choose = (columns == listed).astype(jnp.float32).astype(jnp.bfloat16)
                a = dot(up_h[s], choose, (1, 1))
                b = dot(up_l[s], choose, (1, 1))
                high = a if high is None else high + a
                low_part = b if low_part is None else low_part + b
            picked = (high.astype(jnp.bfloat16), low_part.astype(jnp.bfloat16))
            dst[child, :, pl.ds(base, chunk)] = split_product((inv_h[...], inv_l[...]), picked)
            after(j)

    def end_copy(child, j, target):
        cols = pl.ds(pl.multiple_of(j * chunk, chunk), chunk)
        return pltpu.make_async_remote_copy(
            src_ref=f_end.at[child, :, cols], dst_ref=f_own.at[child, :, cols],
            send_sem=f_send.at[child, j], recv_sem=f_recv.at[child, j],
            device_id=(f, target), device_id_type=MESH,
        )

    server = (t == 1) | (t == n - 2)
    end = lax.div(t - 1, n - 3) * (n - 1)
    aside = lax.rem(t + 1, n)

    def serve(child):
        @pl.when(middle)
        def _():
            split_child(child)

            @pl.when(server)
            def _():
                factor(child, end * width, f_end, lambda j: end_copy(child, j, end).start())

            factor(child, t * width, f_own, lambda j: None)

    def split_factor(child):
        @pl.when(at_end)
        def _():
            @pl.loop(0, width // chunk)
            def _(j):
                end_copy(child, j, aside).wait_recv()

        @pl.loop(0, width // chunk)
        def _(j):
            cols = pl.ds(pl.multiple_of(j * chunk, chunk), chunk)
            high, low_part = parts(f_own[child, :, cols])
            f_h[child, :, cols] = high
            f_l[child, :, cols] = low_part

    lr = low.shape[2]
    tall = stage.shape[0] // lr

    def put(child, shard):
        left = parts(low[child, shard])

        @pl.loop(0, width // chunk)
        def _(j):
            cols = pl.ds(pl.multiple_of(j * chunk, chunk), chunk)
            block = split_product(left, (f_h[child, :, cols], f_l[child, :, cols]))
            for q in range(chunk // 128):
                strip = pl.ds(j * (chunk // 128) + q, lr, stride=tall)
                stage[strip, :] = block[:, q * 128:(q + 1) * 128]

        copy = pltpu.make_async_copy(stage, u_out.at[child, shard], out_sem)
        copy.start()
        copy.wait()

    def index_rows():
        shape = (8, count)
        place = lax.broadcasted_iota(jnp.int32, shape, 1)
        which = lax.broadcasted_iota(jnp.int32, shape, 0)
        digits = jnp.where(which == 0, place >> 7, jnp.where(which == 1, place & 127, 1))
        digits = digits.astype(jnp.float32).astype(jnp.bfloat16)
        span = min(256, index_out.shape[2])
        for child in range(2):
            @pl.loop(0, index_out.shape[2] // span)
            def _(j):
                base = pl.multiple_of(j * span, span)
                rows = lax.broadcasted_iota(jnp.int32, (span, count), 0) + base
                choose = (rows == map_ref[child]).astype(jnp.float32).astype(jnp.bfloat16)
                found = dot(digits, choose, (1, 1)).astype(jnp.int32)
                source = found[0:1] * 128 + found[1:2] + child * count
                index_out[child, :, pl.ds(base, span)] = jnp.where(found[2:3] > 0, source, 2 * count)

    for kind in range(3):
        exchange(kind).start()
        local(kind).start()
    for kind in range(3):
        local(kind).wait()
    send_own(0, 0)
    send_own(1, 0)

    @pl.when(t == n - 2)
    def _():
        hop(2, 0, t, 0).start()

    @pl.when(t == 1)
    def _():
        hop(2, 0, t, 1).start()

    for kind in range(3):
        exchange(kind).wait()

    @pl.when(t == n - 2)
    def _():
        hop(2, 1, t, 0).start()

    @pl.when(t == 1)
    def _():
        hop(2, 1, t, 1).start()

    index_rows()

    @pl.loop(1, n)
    def _(d):
        relay((0, 1), 0, d)

    send_own(0, 1)
    send_own(1, 1)
    serve(0)

    @pl.loop(1, n)
    def _(d):
        relay((0, 1), 1, d)

    for child in range(2):
        @pl.when((t < n - 1) & (t != n - 2))
        def _():
            hop(2, child, t, 0).start()

        @pl.when((t > 0) & (t != 1))
        def _():
            hop(2, child, t, 1).start()

    serve(1)
    for child in range(2):
        split_factor(child)

    @pl.loop(0, 2)
    def _(child):
        put(child, t)

    @pl.loop(1, n)
    def _(d):
        @pl.loop(0, 2)
        def _(child):
            relay((2,), child, d)

            @pl.when(t - d >= 0)
            def _():
                put(child, t - d)

            @pl.when(t + d <= n - 1)
            def _():
                put(child, t + d)

    for child in range(2):
        @pl.loop(0, n)
        def _(s):
            for side in range(2):
                for kind in range(3):
                    @pl.when(takes(kind, side) & (s <= t if side == 0 else s >= t))
                    def _():
                        hop(kind, child, s, side).wait_send()

        @pl.when(server)
        def _():
            @pl.loop(0, width // chunk)
            def _(j):
                end_copy(child, j, aside).wait_send()


def gathered_updates(inverse, upper, lower, maps, n, order, width):
    pivots = inverse.shape[2]
    kr, wc, lr = inverse.shape[1], upper.shape[2], lower.shape[1]
    vmem = pltpu.VMEM
    dma = pltpu.SemaphoreType.DMA
    f32, b16 = jnp.float32, jnp.bfloat16
    chunks = width // min(256, width)
    tall = -(-width // 1024) * 8
    return pl.pallas_call(
        functools.partial(update_kernel, n),
        out_shape=(
            jax.ShapeDtypeStruct((2, n, lr * tall, 128), f32),
            jax.ShapeDtypeStruct((2, 1, order), jnp.int32),
        ),
        in_specs=[pl.BlockSpec(memory_space=pl.ANY)] * 3 + [pl.BlockSpec(memory_space=vmem)],
        out_specs=(pl.BlockSpec(memory_space=pl.ANY), pl.BlockSpec(memory_space=vmem)),
        scratch_shapes=[
            vmem((2, n, pivots, wc), f32),
            vmem((2, n, kr, pivots), f32),
            vmem((2, n, lr, pivots), f32),
            vmem((n, pivots, wc), b16),
            vmem((n, pivots, wc), b16),
            vmem((n * kr, pivots), b16),
            vmem((n * kr, pivots), b16),
            vmem((2, pivots, width), f32),
            vmem((2, pivots, width), f32),
            vmem((2, pivots, width), b16),
            vmem((2, pivots, width), b16),
            vmem((lr * tall, 128), f32),
            dma((3,)), dma((3,)), dma((3,)),
            dma((2, 2, n)), dma((2, n)),
            dma((2, 2, n)), dma((2, n)),
            dma((2, 2, n)), dma((2, n)),
            dma((2, chunks)), dma((2, chunks)), dma,
        ],
        compiler_params=pltpu.CompilerParams(
            collective_id=0, has_side_effects=True, vmem_limit_bytes=56 * 1024 * 1024
        ),
    )(inverse, upper, lower, maps)


def place_kernel(index_ref, base_ref, u_ref, out_ref, u, rows, sem):
    block, width = base_ref.shape
    order = block * pl.num_programs(0)
    total = u_ref.shape[0]
    tall = rows.shape[0] // block
    start = pl.program_id(0) * block

    @pl.when(pl.program_id(0) == 0)
    def _():
        copy = pltpu.make_async_copy(u_ref, u.at[pl.ds(0, total)], sem)
        copy.start()
        u[pl.ds(total, tall), :] = jnp.zeros((tall, 128), jnp.float32)
        copy.wait()

    @pl.loop(0, block // 8)
    def _(i):
        for j in range(8):
            r = i * 8 + j
            a = u[pl.ds(pl.multiple_of(index_ref[start + r] * tall, tall), tall), :]
            b = u[pl.ds(pl.multiple_of(index_ref[order + start + r] * tall, tall), tall), :]
            rows[pl.ds(pl.multiple_of(r * tall, tall), tall), :] = a + b

    for q in range(width // 128):
        cols = slice(q * 128, (q + 1) * 128)
        out_ref[:, cols] = base_ref[:, cols] - rows[pl.ds(q, block, stride=tall), :]


def placed(base, updates, index):
    order, width = base.shape
    block = min(256, order)
    tall = -(-width // 1024) * 8
    return pl.pallas_call(
        place_kernel,
        out_shape=jax.ShapeDtypeStruct(base.shape, base.dtype),
        grid_spec=pltpu.PrefetchScalarGridSpec(
            num_scalar_prefetch=1,
            grid=(order // block,),
            in_specs=[
                pl.BlockSpec((block, width), lambda i, *_: (i, 0)),
                pl.BlockSpec(memory_space=pl.ANY),
            ],
            out_specs=pl.BlockSpec((block, width), lambda i, *_: (i, 0)),
            scratch_shapes=[
                pltpu.VMEM((updates.shape[0] + tall, 128), jnp.float32),
                pltpu.VMEM((block * tall, 128), jnp.float32),
                pltpu.SemaphoreType.DMA,
            ],
        ),
        compiler_params=pltpu.CompilerParams(vmem_limit_bytes=40 * 1024 * 1024),
    )(index, base, updates)


def shards(pivot_inverse, panel_upper, panel_lower, index_map, parent_base):
    base = parent_base[0]
    order, width = base.shape
    n = lax.axis_size("tile")
    group = lax.axis_index("front")
    partner = jnp.bitwise_xor(group, 1)
    maps = jnp.stack([
        lax.dynamic_index_in_dim(index_map, group, 0, keepdims=False)[0],
        lax.dynamic_index_in_dim(index_map, partner, 0, keepdims=False)[1],
    ])
    updates, index = gathered_updates(
        pivot_inverse[0], panel_upper[0], panel_lower[0], maps[:, None, :], n, order, width
    )
    return placed(base, updates.reshape(-1, 128), index.reshape(-1))[None]


def solution(mesh):
    return jax.shard_map(
        shards,
        mesh=mesh,
        in_specs=(
            P("front", None, "tile", None),
            P("front", None, None, "tile"),
            P("front", None, "tile", None),
            P(),
            P("front", None, "tile"),
        ),
        out_specs=P("front", None, "tile"),
        check_vma=False,
    )
```

```python
import functools

import jax
import jax.numpy as jnp
from jax import lax
from jax.experimental import pallas as pl
from jax.experimental.pallas import tpu as pltpu
from jax.sharding import PartitionSpec as P

MESH = pl.DeviceIdType.MESH


def parts(value):
    high = value.astype(jnp.bfloat16)
    return high, (value - high.astype(jnp.float32)).astype(jnp.bfloat16)


def dot(left, right, contract=(1, 0)):
    dims = (((contract[0],), (contract[1],)), ((), ()))
    return lax.dot_general(left, right, dims, preferred_element_type=jnp.float32)


def split_product(left, right):
    total = dot(left[0], right[0])
    total = total + dot(left[0], right[1])
    return total + dot(left[1], right[0])


def update_kernel(
    n, inv_in, up_in, low_in, map_ref, u_out, index_out,
    up, inv, low, up_h, up_l, inv_h, inv_l, f_end, f_own, f_h, f_l, stage,
    local_sem, part_send, part_recv, up_send, up_recv, inv_send, inv_recv,
    low_send, low_recv, f_send, f_recv, out_sem,
):
    t = lax.axis_index("tile")
    f = lax.axis_index("front")
    partner = lax.rem(f, 2) * -2 + 1 + f
    count = map_ref.shape[2]
    wc = up.shape[3]
    kr = inv.shape[2]
    width = f_own.shape[2]
    chunk = min(256, width)
    middle = (t >= 1) & (t <= n - 2)
    at_end = (t == 0) | (t == n - 1)

    barrier = pltpu.get_barrier_semaphore()
    pl.semaphore_signal(barrier, inc=1, device_id=(partner, t), device_id_type=MESH)

    @pl.when(t > 0)
    def _():
        pl.semaphore_signal(barrier, inc=1, device_id=(f, t - 1), device_id_type=MESH)

    @pl.when(t < n - 1)
    def _():
        pl.semaphore_signal(barrier, inc=1, device_id=(f, t + 1), device_id_type=MESH)

    @pl.when(at_end)
    def _():
        pl.semaphore_wait(barrier, 2)

    @pl.when(middle)
    def _():
        pl.semaphore_wait(barrier, 3)

    sources = (up_in, inv_in, low_in)
    targets = (up, inv, low)

    def local(kind):
        return pltpu.make_async_copy(sources[kind].at[0], targets[kind].at[0, t], local_sem.at[kind])

    def exchange(kind):
        return pltpu.make_async_remote_copy(
            src_ref=sources[kind].at[1], dst_ref=targets[kind].at[1, t],
            send_sem=part_send.at[kind], recv_sem=part_recv.at[kind],
            device_id=(partner, t), device_id_type=MESH,
        )

    def hop(kind, child, shard, side):
        send, recv = ((up_send, up_recv), (inv_send, inv_recv), (low_send, low_recv))[kind]
        ref = targets[kind].at[child, shard]
        return pltpu.make_async_remote_copy(
            src_ref=ref, dst_ref=ref,
            send_sem=send.at[side, child, shard], recv_sem=recv.at[child, shard],
            device_id=(f, lax.rem(t + (1 if side == 0 else n - 1), n)), device_id_type=MESH,
        )

    def takes(kind, side):
        if kind == 2:
            return t + 1 <= n - 1 if side == 0 else t - 1 >= 0
        return t + 1 <= n - 2 if side == 0 else t - 1 >= 1

    def send(kind, child, shard, side):
        @pl.when(takes(kind, side))
        def _():
            hop(kind, child, shard, side).start()

    def send_own(kind, child):
        send(kind, child, t, 0)
        send(kind, child, t, 1)

    def relay(kinds, child, d):
        for side, shard, valid in ((0, t - d, t - d >= 0), (1, t + d, t + d <= n - 1)):
            @pl.when(valid & (middle if 0 in kinds else t >= 0))
            def _():
                for kind in kinds:
                    hop(kind, child, shard, side).wait_recv()
                    send(kind, child, shard, side)

    def split_child(child):
        @pl.loop(0, n)
        def _(s):
            high, low_part = parts(up[child, s])
            up_h[child, s] = high
            up_l[child, s] = low_part
            rows = pl.ds(pl.multiple_of(s * kr, kr), kr)
            high, low_part = parts(inv[child, s])
            inv_h[child, rows, :] = high
            inv_l[child, rows, :] = low_part

    def factor(child, start, dst, after):
        @pl.loop(0, width // chunk)
        def _(j):
            base = pl.multiple_of(j * chunk, chunk)
            columns = lax.broadcasted_iota(jnp.int32, (chunk, wc), 0) + (start + base)
            high = low_part = None
            for s in range(n):
                listed = map_ref[child, :, s * wc:(s + 1) * wc]
                choose = (columns == listed).astype(jnp.float32).astype(jnp.bfloat16)
                a = dot(up_h[child, s], choose, (1, 1))
                b = dot(up_l[child, s], choose, (1, 1))
                high = a if high is None else high + a
                low_part = b if low_part is None else low_part + b
            picked = (high.astype(jnp.bfloat16), low_part.astype(jnp.bfloat16))
            dst[child, :, pl.ds(base, chunk)] = split_product((inv_h[child], inv_l[child]), picked)
            after(j)

    def end_copy(child, j, target):
        cols = pl.ds(pl.multiple_of(j * chunk, chunk), chunk)
        return pltpu.make_async_remote_copy(
            src_ref=f_end.at[child, :, cols], dst_ref=f_own.at[child, :, cols],
            send_sem=f_send.at[child, j], recv_sem=f_recv.at[child, j],
            device_id=(f, target), device_id_type=MESH,
        )

    server = (t == 1) | (t == n - 2)
    end = lax.div(t - 1, n - 3) * (n - 1)
    aside = lax.rem(t + 1, n)

    def prepare(child):
        @pl.when(middle)
        def _():
            split_child(child)

            @pl.when(server)
            def _():
                factor(child, end * width, f_end, lambda j: end_copy(child, j, end).start())

    def own(child):
        @pl.when(middle)
        def _():
            factor(child, t * width, f_own, lambda j: None)

    def split_factor(child):
        @pl.when(at_end)
        def _():
            @pl.loop(0, width // chunk)
            def _(j):
                end_copy(child, j, aside).wait_recv()

        @pl.loop(0, width // chunk)
        def _(j):
            cols = pl.ds(pl.multiple_of(j * chunk, chunk), chunk)
            high, low_part = parts(f_own[child, :, cols])
            f_h[child, :, cols] = high
            f_l[child, :, cols] = low_part

    lr = low.shape[2]
    tall = stage.shape[0] // lr

    def put(child, shard):
        left = parts(low[child, shard])

        @pl.loop(0, width // chunk)
        def _(j):
            cols = pl.ds(pl.multiple_of(j * chunk, chunk), chunk)
            block = split_product(left, (f_h[child, :, cols], f_l[child, :, cols]))
            for q in range(chunk // 128):
                strip = pl.ds(j * (chunk // 128) + q, lr, stride=tall)
                stage[strip, :] = block[:, q * 128:(q + 1) * 128]

        copy = pltpu.make_async_copy(stage, u_out.at[child, shard], out_sem)
        copy.start()
        copy.wait()

    def index_rows():
        shape = (8, count)
        place = lax.broadcasted_iota(jnp.int32, shape, 1)
        which = lax.broadcasted_iota(jnp.int32, shape, 0)
        digits = jnp.where(which == 0, place >> 7, jnp.where(which == 1, place & 127, 1))
        digits = digits.astype(jnp.float32).astype(jnp.bfloat16)
        span = min(256, index_out.shape[2])
        for child in range(2):
            @pl.loop(0, index_out.shape[2] // span)
            def _(j):
                base = pl.multiple_of(j * span, span)
                rows = lax.broadcasted_iota(jnp.int32, (span, count), 0) + base
                choose = (rows == map_ref[child]).astype(jnp.float32).astype(jnp.bfloat16)
                found = dot(digits, choose, (1, 1)).astype(jnp.int32)
                source = found[0:1] * 128 + found[1:2] + child * count
                index_out[child, :, pl.ds(base, span)] = jnp.where(found[2:3] > 0, source, 2 * count) * tall

    for kind in range(3):
        exchange(kind).start()
        local(kind).start()
    for kind in range(3):
        local(kind).wait()
    send_own(0, 0)
    send_own(1, 0)

    @pl.when(t == n - 2)
    def _():
        hop(2, 0, t, 0).start()

    @pl.when(t == 1)
    def _():
        hop(2, 0, t, 1).start()

    for kind in range(3):
        exchange(kind).wait()

    @pl.when(t == n - 2)
    def _():
        hop(2, 1, t, 0).start()

    @pl.when(t == 1)
    def _():
        hop(2, 1, t, 1).start()

    relay((0, 1), 0, 1)
    send_own(0, 1)
    send_own(1, 1)
    index_rows()

    @pl.loop(2, n)
    def _(d):
        relay((0, 1), 0, d)

    prepare(0)
    relay((0, 1), 1, 1)

    for child in range(2):
        @pl.when((t < n - 1) & (t != n - 2))
        def _():
            hop(2, child, t, 0).start()

        @pl.when((t > 0) & (t != 1))
        def _():
            hop(2, child, t, 1).start()

    own(0)

    @pl.loop(2, n)
    def _(d):
        relay((0, 1), 1, d)

    prepare(1)
    own(1)
    for child in range(2):
        split_factor(child)

    @pl.loop(0, 2)
    def _(child):
        put(child, t)

    @pl.loop(1, n)
    def _(d):
        @pl.loop(0, 2)
        def _(child):
            relay((2,), child, d)

            @pl.when(t - d >= 0)
            def _():
                put(child, t - d)

            @pl.when(t + d <= n - 1)
            def _():
                put(child, t + d)

    for child in range(2):
        @pl.loop(0, n)
        def _(s):
            for side in range(2):
                for kind in range(3):
                    @pl.when(takes(kind, side) & (s <= t if side == 0 else s >= t))
                    def _():
                        hop(kind, child, s, side).wait_send()

        @pl.when(server)
        def _():
            @pl.loop(0, width // chunk)
            def _(j):
                end_copy(child, j, aside).wait_send()


def gathered_updates(inverse, upper, lower, maps, n, order, width):
    pivots = inverse.shape[2]
    kr, wc, lr = inverse.shape[1], upper.shape[2], lower.shape[1]
    vmem = pltpu.VMEM
    dma = pltpu.SemaphoreType.DMA
    f32, b16 = jnp.float32, jnp.bfloat16
    chunks = width // min(256, width)
    tall = -(-width // 1024) * 8
    return pl.pallas_call(
        functools.partial(update_kernel, n),
        out_shape=(
            jax.ShapeDtypeStruct((2, n, lr * tall, 128), f32),
            jax.ShapeDtypeStruct((2, 1, order), jnp.int32),
        ),
        in_specs=[pl.BlockSpec(memory_space=pl.ANY)] * 3 + [pl.BlockSpec(memory_space=vmem)],
        out_specs=(pl.BlockSpec(memory_space=pl.ANY), pl.BlockSpec(memory_space=vmem)),
        scratch_shapes=[
            vmem((2, n, pivots, wc), f32),
            vmem((2, n, kr, pivots), f32),
            vmem((2, n, lr, pivots), f32),
            vmem((2, n, pivots, wc), b16),
            vmem((2, n, pivots, wc), b16),
            vmem((2, n * kr, pivots), b16),
            vmem((2, n * kr, pivots), b16),
            vmem((2, pivots, width), f32),
            vmem((2, pivots, width), f32),
            vmem((2, pivots, width), b16),
            vmem((2, pivots, width), b16),
            vmem((lr * tall, 128), f32),
            dma((3,)), dma((3,)), dma((3,)),
            dma((2, 2, n)), dma((2, n)),
            dma((2, 2, n)), dma((2, n)),
            dma((2, 2, n)), dma((2, n)),
            dma((2, chunks)), dma((2, chunks)), dma,
        ],
        compiler_params=pltpu.CompilerParams(
            collective_id=0, has_side_effects=True, vmem_limit_bytes=56 * 1024 * 1024
        ),
    )(inverse, upper, lower, maps)


def place_kernel(index_ref, base_ref, u_ref, out_ref, u, rows, sem):
    block, width = base_ref.shape
    order = block * pl.num_programs(0)
    total = u_ref.shape[0]
    tall = rows.shape[0] // block
    start = pl.program_id(0) * block

    @pl.when(pl.program_id(0) == 0)
    def _():
        copy = pltpu.make_async_copy(u_ref, u.at[pl.ds(0, total)], sem)
        copy.start()
        u[pl.ds(total, tall), :] = jnp.zeros((tall, 128), jnp.float32)
        copy.wait()

    turn = 32

    @pl.loop(0, block // turn)
    def _(i):
        for j in range(turn):
            r = i * turn + j
            a = u[pl.ds(pl.multiple_of(index_ref[start + r], tall), tall), :]
            b = u[pl.ds(pl.multiple_of(index_ref[order + start + r], tall), tall), :]
            rows[pl.ds(pl.multiple_of(r * tall, tall), tall), :] = a + b

    for q in range(width // 128):
        cols = slice(q * 128, (q + 1) * 128)
        out_ref[:, cols] = base_ref[:, cols] - rows[pl.ds(q, block, stride=tall), :]


def placed(base, updates, index):
    order, width = base.shape
    block = min(256, order)
    tall = -(-width // 1024) * 8
    return pl.pallas_call(
        place_kernel,
        out_shape=jax.ShapeDtypeStruct(base.shape, base.dtype),
        grid_spec=pltpu.PrefetchScalarGridSpec(
            num_scalar_prefetch=1,
            grid=(order // block,),
            in_specs=[
                pl.BlockSpec((block, width), lambda i, *_: (i, 0)),
                pl.BlockSpec(memory_space=pl.ANY),
            ],
            out_specs=pl.BlockSpec((block, width), lambda i, *_: (i, 0)),
            scratch_shapes=[
                pltpu.VMEM((updates.shape[0] + tall, 128), jnp.float32),
                pltpu.VMEM((block * tall, 128), jnp.float32),
                pltpu.SemaphoreType.DMA,
            ],
        ),
        compiler_params=pltpu.CompilerParams(vmem_limit_bytes=40 * 1024 * 1024),
    )(index, base, updates)


def shards(pivot_inverse, panel_upper, panel_lower, index_map, parent_base):
    base = parent_base[0]
    order, width = base.shape
    n = lax.axis_size("tile")
    group = lax.axis_index("front")
    partner = jnp.bitwise_xor(group, 1)
    maps = jnp.stack([
        lax.dynamic_index_in_dim(index_map, group, 0, keepdims=False)[0],
        lax.dynamic_index_in_dim(index_map, partner, 0, keepdims=False)[1],
    ])
    updates, index = gathered_updates(
        pivot_inverse[0], panel_upper[0], panel_lower[0], maps[:, None, :], n, order, width
    )
    return placed(base, updates.reshape(-1, 128), index.reshape(-1))[None]


def solution(mesh):
    return jax.shard_map(
        shards,
        mesh=mesh,
        in_specs=(
            P("front", None, "tile", None),
            P("front", None, None, "tile"),
            P("front", None, "tile", None),
            P(),
            P("front", None, "tile"),
        ),
        out_specs=P("front", None, "tile"),
        check_vma=False,
    )
```

```python
import functools

import jax
import jax.numpy as jnp
from jax import lax
from jax.experimental import pallas as pl
from jax.experimental.pallas import tpu as pltpu
from jax.sharding import PartitionSpec as P

MESH = pl.DeviceIdType.MESH


def parts(value):
    high = value.astype(jnp.bfloat16)
    return high, (value - high.astype(jnp.float32)).astype(jnp.bfloat16)


def dot(left, right, contract=(1, 0)):
    dims = (((contract[0],), (contract[1],)), ((), ()))
    return lax.dot_general(left, right, dims, preferred_element_type=jnp.float32)


def split_product(left, right):
    total = dot(left[0], right[0])
    total = total + dot(left[0], right[1])
    return total + dot(left[1], right[0])


def update_kernel(
    n, inv_in, up_in, low_in, map_ref, u_out, index_out,
    up, inv, low, up_h, up_l, inv_h, inv_l, f_end, f_own, f_h, f_l, stage,
    local_sem, part_send, part_recv, up_send, up_recv, inv_send, inv_recv,
    low_send, low_recv, f_send, f_recv, out_sem,
):
    t = lax.axis_index("tile")
    f = lax.axis_index("front")
    partner = lax.rem(f, 2) * -2 + 1 + f
    count = map_ref.shape[2]
    wc = up.shape[3]
    kr = inv.shape[2]
    width = f_own.shape[2]
    chunk = min(256, width)
    middle = (t >= 1) & (t <= n - 2)
    at_end = (t == 0) | (t == n - 1)

    barrier = pltpu.get_barrier_semaphore()
    pl.semaphore_signal(barrier, inc=1, device_id=(partner, t), device_id_type=MESH)

    @pl.when(t > 0)
    def _():
        pl.semaphore_signal(barrier, inc=1, device_id=(f, t - 1), device_id_type=MESH)

    @pl.when(t < n - 1)
    def _():
        pl.semaphore_signal(barrier, inc=1, device_id=(f, t + 1), device_id_type=MESH)

    @pl.when(at_end)
    def _():
        pl.semaphore_wait(barrier, 2)

    @pl.when(middle)
    def _():
        pl.semaphore_wait(barrier, 3)

    sources = (up_in, inv_in, low_in)
    targets = (up, inv, low)

    def local(kind):
        return pltpu.make_async_copy(sources[kind].at[0], targets[kind].at[0, t], local_sem.at[kind])

    def exchange(kind):
        return pltpu.make_async_remote_copy(
            src_ref=sources[kind].at[1], dst_ref=targets[kind].at[1, t],
            send_sem=part_send.at[kind], recv_sem=part_recv.at[kind],
            device_id=(partner, t), device_id_type=MESH,
        )

    def hop(kind, child, shard, side):
        send, recv = ((up_send, up_recv), (inv_send, inv_recv), (low_send, low_recv))[kind]
        ref = targets[kind].at[child, shard]
        return pltpu.make_async_remote_copy(
            src_ref=ref, dst_ref=ref,
            send_sem=send.at[side, child, shard], recv_sem=recv.at[child, shard],
            device_id=(f, lax.rem(t + (1 if side == 0 else n - 1), n)), device_id_type=MESH,
        )

    def takes(kind, side):
        if kind == 2:
            return t + 1 <= n - 1 if side == 0 else t - 1 >= 0
        return t + 1 <= n - 2 if side == 0 else t - 1 >= 1

    def send(kind, child, shard, side):
        @pl.when(takes(kind, side))
        def _():
            hop(kind, child, shard, side).start()

    def send_own(kind, child):
        send(kind, child, t, 0)
        send(kind, child, t, 1)

    def relay(kinds, child, d):
        for side, shard, valid in ((0, t - d, t - d >= 0), (1, t + d, t + d <= n - 1)):
            @pl.when(valid & (middle if 0 in kinds else t >= 0))
            def _():
                for kind in kinds:
                    hop(kind, child, shard, side).wait_recv()
                    send(kind, child, shard, side)

    def split_child(child):
        @pl.loop(0, n)
        def _(s):
            high, low_part = parts(up[child, s])
            up_h[s] = high
            up_l[s] = low_part
            rows = pl.ds(pl.multiple_of(s * kr, kr), kr)
            high, low_part = parts(inv[child, s])
            inv_h[rows, :] = high
            inv_l[rows, :] = low_part

    def factor(child, start, dst, after):
        @pl.loop(0, width // chunk)
        def _(j):
            base = pl.multiple_of(j * chunk, chunk)
            columns = lax.broadcasted_iota(jnp.int32, (chunk, wc), 0) + (start + base)
            high = low_part = None
            for s in range(n):
                listed = map_ref[child, :, s * wc:(s + 1) * wc]
                choose = (columns == listed).astype(jnp.float32).astype(jnp.bfloat16)
                a = dot(up_h[s], choose, (1, 1))
                b = dot(up_l[s], choose, (1, 1))
                high = a if high is None else high + a
                low_part = b if low_part is None else low_part + b
            picked = (high.astype(jnp.bfloat16), low_part.astype(jnp.bfloat16))
            dst[child, :, pl.ds(base, chunk)] = split_product((inv_h[...], inv_l[...]), picked)
            after(j)

    def end_copy(child, j, target):
        cols = pl.ds(pl.multiple_of(j * chunk, chunk), chunk)
        return pltpu.make_async_remote_copy(
            src_ref=f_end.at[child, :, cols], dst_ref=f_own.at[child, :, cols],
            send_sem=f_send.at[child, j], recv_sem=f_recv.at[child, j],
            device_id=(f, target), device_id_type=MESH,
        )

    server = (t == 1) | (t == n - 2)
    end = lax.div(t - 1, n - 3) * (n - 1)
    aside = lax.rem(t + 1, n)

    def serve(child):
        @pl.when(middle)
        def _():
            split_child(child)

            @pl.when(server)
            def _():
                factor(child, end * width, f_end, lambda j: end_copy(child, j, end).start())

            factor(child, t * width, f_own, lambda j: None)

    def split_factor(child):
        @pl.when(at_end)
        def _():
            @pl.loop(0, width // chunk)
            def _(j):
                end_copy(child, j, aside).wait_recv()

        @pl.loop(0, width // chunk)
        def _(j):
            cols = pl.ds(pl.multiple_of(j * chunk, chunk), chunk)
            high, low_part = parts(f_own[child, :, cols])
            f_h[child, :, cols] = high
            f_l[child, :, cols] = low_part

    lr = low.shape[2]
    tall = stage.shape[0] // lr

    def put(child, shard):
        left = parts(low[child, shard])

        @pl.loop(0, width // chunk)
        def _(j):
            cols = pl.ds(pl.multiple_of(j * chunk, chunk), chunk)
            block = split_product(left, (f_h[child, :, cols], f_l[child, :, cols]))
            for q in range(chunk // 128):
                strip = pl.ds(j * (chunk // 128) + q, lr, stride=tall)
                stage[strip, :] = block[:, q * 128:(q + 1) * 128]

        copy = pltpu.make_async_copy(stage, u_out.at[child, shard], out_sem)
        copy.start()
        copy.wait()

    def index_rows():
        shape = (8, count)
        place = lax.broadcasted_iota(jnp.int32, shape, 1)
        which = lax.broadcasted_iota(jnp.int32, shape, 0)
        digits = jnp.where(which == 0, place >> 7, jnp.where(which == 1, place & 127, 1))
        digits = digits.astype(jnp.float32).astype(jnp.bfloat16)
        span = min(256, index_out.shape[2])
        for child in range(2):
            @pl.loop(0, index_out.shape[2] // span)
            def _(j):
                base = pl.multiple_of(j * span, span)
                rows = lax.broadcasted_iota(jnp.int32, (span, count), 0) + base
                choose = (rows == map_ref[child]).astype(jnp.float32).astype(jnp.bfloat16)
                found = dot(digits, choose, (1, 1)).astype(jnp.int32)
                source = found[0:1] * 128 + found[1:2] + child * count
                index_out[child, :, pl.ds(base, span)] = jnp.where(found[2:3] > 0, source, 2 * count)

    for kind in range(3):
        exchange(kind).start()
        local(kind).start()
    for kind in range(3):
        local(kind).wait()
    send_own(0, 0)
    send_own(1, 0)

    @pl.when(t == n - 2)
    def _():
        hop(2, 0, t, 0).start()

    @pl.when(t == 1)
    def _():
        hop(2, 0, t, 1).start()

    for kind in range(3):
        exchange(kind).wait()

    @pl.when(t == n - 2)
    def _():
        hop(2, 1, t, 0).start()

    @pl.when(t == 1)
    def _():
        hop(2, 1, t, 1).start()

    index_rows()

    @pl.loop(1, n)
    def _(d):
        relay((0, 1), 0, d)

    send_own(0, 1)
    send_own(1, 1)
    serve(0)

    @pl.loop(1, n)
    def _(d):
        relay((0, 1), 1, d)

    for child in range(2):
        @pl.when((t < n - 1) & (t != n - 2))
        def _():
            hop(2, child, t, 0).start()

        @pl.when((t > 0) & (t != 1))
        def _():
            hop(2, child, t, 1).start()

    serve(1)
    for child in range(2):
        split_factor(child)

    @pl.loop(0, 2)
    def _(child):
        put(child, t)

    @pl.loop(1, n)
    def _(d):
        @pl.loop(0, 2)
        def _(child):
            relay((2,), child, d)

            @pl.when(t - d >= 0)
            def _():
                put(child, t - d)

            @pl.when(t + d <= n - 1)
            def _():
                put(child, t + d)

    for child in range(2):
        @pl.loop(0, n)
        def _(s):
            for side in range(2):
                for kind in range(3):
                    @pl.when(takes(kind, side) & (s <= t if side == 0 else s >= t))
                    def _():
                        hop(kind, child, s, side).wait_send()

        @pl.when(server)
        def _():
            @pl.loop(0, width // chunk)
            def _(j):
                end_copy(child, j, aside).wait_send()


def gathered_updates(inverse, upper, lower, maps, n, order, width):
    pivots = inverse.shape[2]
    kr, wc, lr = inverse.shape[1], upper.shape[2], lower.shape[1]
    vmem = pltpu.VMEM
    dma = pltpu.SemaphoreType.DMA
    f32, b16 = jnp.float32, jnp.bfloat16
    chunks = width // min(256, width)
    tall = -(-width // 1024) * 8
    return pl.pallas_call(
        functools.partial(update_kernel, n),
        out_shape=(
            jax.ShapeDtypeStruct((2, n, lr * tall, 128), f32),
            jax.ShapeDtypeStruct((2, 1, order), jnp.int32),
        ),
        in_specs=[pl.BlockSpec(memory_space=pl.ANY)] * 3 + [pl.BlockSpec(memory_space=vmem)],
        out_specs=(pl.BlockSpec(memory_space=pl.ANY), pl.BlockSpec(memory_space=vmem)),
        scratch_shapes=[
            vmem((2, n, pivots, wc), f32),
            vmem((2, n, kr, pivots), f32),
            vmem((2, n, lr, pivots), f32),
            vmem((n, pivots, wc), b16),
            vmem((n, pivots, wc), b16),
            vmem((n * kr, pivots), b16),
            vmem((n * kr, pivots), b16),
            vmem((2, pivots, width), f32),
            vmem((2, pivots, width), f32),
            vmem((2, pivots, width), b16),
            vmem((2, pivots, width), b16),
            vmem((lr * tall, 128), f32),
            dma((3,)), dma((3,)), dma((3,)),
            dma((2, 2, n)), dma((2, n)),
            dma((2, 2, n)), dma((2, n)),
            dma((2, 2, n)), dma((2, n)),
            dma((2, chunks)), dma((2, chunks)), dma,
        ],
        compiler_params=pltpu.CompilerParams(
            collective_id=0, has_side_effects=True, vmem_limit_bytes=56 * 1024 * 1024
        ),
    )(inverse, upper, lower, maps)


def place_kernel(index_ref, base_ref, u_ref, out_ref, u, rows, sem):
    block, width = base_ref.shape
    order = block * pl.num_programs(0)
    total = u_ref.shape[0]
    tall = rows.shape[0] // block
    start = pl.program_id(0) * block

    @pl.when(pl.program_id(0) == 0)
    def _():
        copy = pltpu.make_async_copy(u_ref, u.at[pl.ds(0, total)], sem)
        copy.start()
        u[pl.ds(total, tall), :] = jnp.zeros((tall, 128), jnp.float32)
        copy.wait()

    turn = 32

    @pl.loop(0, block // turn)
    def _(i):
        for j in range(turn):
            r = i * turn + j
            a = u[pl.ds(pl.multiple_of(index_ref[start + r] * tall, tall), tall), :]
            b = u[pl.ds(pl.multiple_of(index_ref[order + start + r] * tall, tall), tall), :]
            rows[pl.ds(pl.multiple_of(r * tall, tall), tall), :] = a + b

    for q in range(width // 128):
        cols = slice(q * 128, (q + 1) * 128)
        out_ref[:, cols] = base_ref[:, cols] - rows[pl.ds(q, block, stride=tall), :]


def placed(base, updates, index):
    order, width = base.shape
    block = min(256, order)
    tall = -(-width // 1024) * 8
    return pl.pallas_call(
        place_kernel,
        out_shape=jax.ShapeDtypeStruct(base.shape, base.dtype),
        grid_spec=pltpu.PrefetchScalarGridSpec(
            num_scalar_prefetch=1,
            grid=(order // block,),
            in_specs=[
                pl.BlockSpec((block, width), lambda i, *_: (i, 0)),
                pl.BlockSpec(memory_space=pl.ANY),
            ],
            out_specs=pl.BlockSpec((block, width), lambda i, *_: (i, 0)),
            scratch_shapes=[
                pltpu.VMEM((updates.shape[0] + tall, 128), jnp.float32),
                pltpu.VMEM((block * tall, 128), jnp.float32),
                pltpu.SemaphoreType.DMA,
            ],
        ),
        compiler_params=pltpu.CompilerParams(vmem_limit_bytes=40 * 1024 * 1024),
    )(index, base, updates)


def shards(pivot_inverse, panel_upper, panel_lower, index_map, parent_base):
    base = parent_base[0]
    order, width = base.shape
    n = lax.axis_size("tile")
    group = lax.axis_index("front")
    partner = jnp.bitwise_xor(group, 1)
    maps = jnp.stack([
        lax.dynamic_index_in_dim(index_map, group, 0, keepdims=False)[0],
        lax.dynamic_index_in_dim(index_map, partner, 0, keepdims=False)[1],
    ])
    updates, index = gathered_updates(
        pivot_inverse[0], panel_upper[0], panel_lower[0], maps[:, None, :], n, order, width
    )
    return placed(base, updates.reshape(-1, 128), index.reshape(-1))[None]


def solution(mesh):
    return jax.shard_map(
        shards,
        mesh=mesh,
        in_specs=(
            P("front", None, "tile", None),
            P("front", None, None, "tile"),
            P("front", None, "tile", None),
            P(),
            P("front", None, "tile"),
        ),
        out_specs=P("front", None, "tile"),
        check_vma=False,
    )
```
